32 devices in a mesh: groups: 2 (over x), seq: 16 (over z, y, core).
Axes of the slice: x: 2, y: 2, z: 4, core: 2. Of those that a mesh axis runs over, the one named last changes fastest.
Arguments:
- tokens: bfloat16 [1024, 512, 512], P(('groups', 'seq')), parts along dimension 0, may hold values from -6 to 6
- cotangent: bfloat16 [1024, 512, 512], P('groups', 'seq'), parts along dimension 0, may hold values from -6 to 6
- w_first: bfloat16 [512, 512], P('seq'), may hold values from -0.25 to 0.25
- w_second: bfloat16 [512, 512], P('seq'), may hold values from -0.25 to 0.25
- mask_first: int32 [4, 4], replicated, may hold values from 0 to 1, as said below
- mask_second: int32 [4, 4], replicated, may hold values from 0 to 1, as said below
- gate_values: bfloat16 [1024, 512], P(('groups', 'seq')), parts along dimension 0, may hold values from -4 to 4
Outputs:
- grad_tokens: bfloat16 [1024, 512, 512], P(('groups', 'seq')), parts along dimension 0
- grad_first: float32 [1024, 512], P(('groups', 'seq')), parts along dimension 0
- grad_second: float32 [1024, 512], P(('groups', 'seq')), parts along dimension 0
The draws below stay inside these ranges and needn't reach their ends.
There are 2 independent parts, one for each index of `groups`. The reference program is written for one: setup_inputs(seed, part) draws one part's arguments, and reference() takes and returns one part's arrays. A program takes and returns all parts, laid end to end along the dimension named above; an argument that names none is the same for every part. Nothing has to cross between parts.
Inputs may be any that keep to these rules, and one draw needn't show every extreme that they name: `mask_first`: the diagonal blocks of each factor are always kept. `mask_second`: the diagonal blocks of each factor are always kept.
All inputs are finite; a program needn't handle non-finite values.
Results may differ from the reference program's by a relative error of at most 0.0054.
Values may be sent and summed in bfloat16 or wider, within the bound.
A program may use at most 320 MiB of HBM per device.

```python
import math
import jax
import jax.numpy as jnp

S = 512
C = 512
BLK = 128
NB = 4


def block_mask(key):
    chosen = jax.random.randint(key, (NB, NB), 0, 2)
    labels = jnp.arange(NB, dtype=jnp.int32)
    diagonal = labels[:, None] == labels[None, :]
    return jnp.where(diagonal, 1, chosen).astype(jnp.int32)


def draw_mask_first(key, part):
    return block_mask(jax.random.fold_in(key, 11))


def draw_mask_second(key, part):
    return block_mask(jax.random.fold_in(key, 23))


def raised(values, stream_key, source, target, blocks, factor):
    def block_of(axis_at):
        return (jnp.arange(values.shape[axis_at]) // (values.shape[axis_at] // blocks)).reshape((-1,) + (1,) * (values.ndim - 1 - axis_at))

    near = jax.random.permutation(stream_key, blocks)[block_of(target)]
    other_side = (block_of(target) + blocks // 2) % blocks
    return jnp.where((block_of(source) == near) | (block_of(source) == other_side), factor * values, values)


def level_of(stream_key, extent, cuts, least, largest):
    level = 1.0
    for axis_at, shards_of in cuts:
        steps = jax.random.uniform(jax.random.fold_in(jax.random.fold_in(stream_key, 6), axis_at), (shards_of,), jnp.float32, least / len(cuts), largest / len(cuts))
        level = level * jnp.repeat(jnp.exp(steps), extent[axis_at] // shards_of).reshape((-1,) + (1,) * (len(extent) - 1 - axis_at))
    return level


def bell_draw(own_key, shape, width, limit, cuts=(), kind=jnp.bfloat16):
    entries = width * jax.random.normal(own_key, shape, jnp.float32)
    if cuts:
        entries = entries * level_of(own_key, shape, cuts, -0.22, 0.18)
    return jnp.clip(entries, -limit, limit).astype(kind)


def noise_with(own_key, extent, scale, reach, shards, heavy, kind=jnp.bfloat16):
    drawn = scale * jax.random.normal(own_key, extent, jnp.float32)
    if shards:
        drawn = drawn * level_of(own_key, extent, shards, -0.22, 0.18)
    return jnp.clip(raised(drawn, jax.random.fold_in(own_key, 3), *heavy), -reach, reach).astype(kind)


def setup_inputs(seed: int = 0, part: int = 0) -> dict:
    arg_keys = jax.random.split(jax.random.key(seed), 8)
    part_splits = jax.random.split(jax.random.fold_in(arg_keys[7], part), 8)
    return {
        "tokens": noise_with(part_splits[0], (S, S, C), 1.0, 6.0, ((0, 16),), (0, 1, 16, 2.0)),
        "cotangent": noise_with(part_splits[1], (S, S, C), 1.0, 6.0, ((1, 16),), (1, 0, 16, 2.0)),
        "w_first": bell_draw(arg_keys[2], (S, S), S ** -0.5, 0.25, ((0, 16),)),
        "w_second": bell_draw(arg_keys[3], (S, S), S ** -0.5, 0.25, ((0, 16),)),
        "mask_first": draw_mask_first(jax.random.fold_in(arg_keys[7], 71), part),
        "mask_second": draw_mask_second(jax.random.fold_in(arg_keys[7], 71), part),
        "gate_values": bell_draw(part_splits[6], (S, S), 1.0, 4.0, ((0, 16),)),
    }


def expand_mask(mask):
    blocks = (jnp.arange(S, dtype=jnp.int32) // BLK).astype(jnp.int32)
    return mask[blocks][:, blocks].astype(jnp.float32)

def reference(tokens, cotangent, w_first, w_second, mask_first, mask_second, gate_values):
    keep_first = expand_mask(mask_first)
    keep_second = expand_mask(mask_second)
    w1m = (w_first.astype(jnp.float32) * keep_first).astype(jnp.bfloat16).astype(jnp.float32)
    w2m = (w_second.astype(jnp.float32) * keep_second).astype(jnp.bfloat16).astype(jnp.float32)
    gate_full = gate_values.astype(jnp.float32)
    x_full = tokens.astype(jnp.float32)
    gated = x_full * gate_full[:, :, None]
    hidden = jnp.einsum('ijc,kj->ikc', x_full, w1m)
    mixed = (hidden * gated).astype(jnp.bfloat16).astype(jnp.float32)
    cot_full = cotangent.astype(jnp.float32)
    back_mixed = jnp.einsum('ki,kjc->ijc', w2m, cot_full).astype(jnp.bfloat16).astype(jnp.float32)
    raw_second = jnp.einsum('kjc,ijc->ki', cot_full, mixed)
    back_hidden = (back_mixed * gated).astype(jnp.bfloat16).astype(jnp.float32)
    direct = gate_full[:, :, None] * back_mixed * hidden
    through = jnp.einsum('ikc,kj->ijc', back_hidden, w1m)
    grad_tokens = (direct + through).astype(jnp.bfloat16)
    raw_first = jnp.einsum('ikc,ijc->kj', back_hidden, x_full)
    factor = 1.0 / math.sqrt(S * C)
    grad_first = keep_first * raw_first * factor
    grad_second = keep_second * raw_second * factor
    return (grad_tokens, grad_first, grad_second)
```

```python
import math

import jax
import jax.numpy as jnp
from jax import lax
from jax.sharding import PartitionSpec as P

BLK = 128


def expand_rows(mask, row_ids, extent):
    labels = jnp.arange(mask.shape[0], dtype=jnp.int32)
    row_pick = ((row_ids // BLK)[:, None] == labels[None, :]).astype(jnp.float32)
    col_pick = ((jnp.arange(extent, dtype=jnp.int32) // BLK)[:, None] == labels[None, :]).astype(
        jnp.float32
    )
    return jnp.dot(jnp.dot(row_pick, mask.astype(jnp.float32)), col_pick.T)


def per_device(tokens, cotangent, w_first, w_second, mask_first, mask_second, gate_values):
    position = lax.axis_index("seq")
    extent = tokens.shape[1]
    channels = tokens.shape[2]
    shard_rows = w_first.shape[0]
    row_ids = position * shard_rows + jnp.arange(shard_rows, dtype=jnp.int32)
    keep_first = expand_rows(mask_first, row_ids, extent)
    keep_second = expand_rows(mask_second, row_ids, extent)
    local_first = (w_first.astype(jnp.float32) * keep_first).astype(jnp.bfloat16)
    local_second = (w_second.astype(jnp.float32) * keep_second).astype(jnp.bfloat16)
    full = lax.all_gather(jnp.stack([local_first, local_second]), "seq", axis=1, tiled=True)
    full_first, full_second = full[0], full[1]
    shards = extent // shard_rows
    flat_cot = cotangent.reshape(extent, -1)
    back_flat = lax.dot_general(
        full_second, flat_cot, (((0,), (0,)), ((), ())), preferred_element_type=jnp.float32
    )
    back_col = back_flat.astype(jnp.bfloat16).reshape(cotangent.shape)
    back_rows = lax.all_to_all(back_col, "seq", split_axis=0, concat_axis=1, tiled=True)
    tokens_late, back_col = lax.optimization_barrier((tokens, back_col))
    gate_full = gate_values.astype(jnp.float32)[:, :, None]
    gated = tokens_late.astype(jnp.float32) * gate_full
    hidden = jnp.einsum("ijc,kj->ikc", tokens_late, full_first, preferred_element_type=jnp.float32)
    mixed = (hidden * gated).astype(jnp.bfloat16)
    mixed, back_rows = lax.optimization_barrier((mixed, back_rows))
    columns = lax.all_to_all(mixed, "seq", split_axis=1, concat_axis=0, tiled=True)
    flat_cols = columns.reshape(extent, -1)
    back_float = back_rows.astype(jnp.float32)
    back_hidden = (back_float * gated).astype(jnp.bfloat16)
    direct = gate_full * back_float * hidden
    through = jnp.einsum("ikc,kj->ijc", back_hidden, full_first, preferred_element_type=jnp.float32)
    grad_tokens = (direct + through).astype(jnp.bfloat16)
    summed_first = lax.psum_scatter(
        jnp.einsum("ikc,ijc->kj", back_hidden, tokens_late, preferred_element_type=jnp.float32),
        "seq",
        scatter_dimension=0,
        tiled=True,
    )
    part_second = lax.dot_general(
        flat_cot, flat_cols, (((1,), (1,)), ((), ())), preferred_element_type=jnp.float32
    )
    spread = lax.all_to_all(
        part_second.reshape(shards, shard_rows, extent), "seq", split_axis=0, concat_axis=0, tiled=True
    )
    summed_second = jnp.sum(spread, axis=0)
    factor = 1.0 / math.sqrt(extent * channels)
    grad_first = keep_first * summed_first * factor
    grad_second = keep_second * summed_second * factor
    return (grad_tokens, grad_first, grad_second)


def solution(mesh):
    in_specs = (
        P(("groups", "seq"), None, None),
        P("groups", "seq", None),
        P("seq", None),
        P("seq", None),
        P(),
        P(),
        P(("groups", "seq"), None),
    )
    out_specs = (
        P(("groups", "seq"), None, None),
        P(("groups", "seq"), None),
        P(("groups", "seq"), None),
    )
    return jax.shard_map(
        per_device, mesh=mesh, in_specs=in_specs, out_specs=out_specs, check_vma=False
    )
```

```python
import math

import jax
import jax.numpy as jnp
from jax import lax
from jax.sharding import PartitionSpec as P

BLK = 128


def expand_rows(mask, row_ids, extent):
    labels = jnp.arange(mask.shape[0], dtype=jnp.int32)
    row_pick = ((row_ids // BLK)[:, None] == labels[None, :]).astype(jnp.float32)
    col_pick = ((jnp.arange(extent, dtype=jnp.int32) // BLK)[:, None] == labels[None, :]).astype(
        jnp.float32
    )
    return jnp.dot(jnp.dot(row_pick, mask.astype(jnp.float32)), col_pick.T)


def per_device(tokens, cotangent, w_first, w_second, mask_first, mask_second, gate_values):
    position = lax.axis_index("seq")
    extent = tokens.shape[1]
    channels = tokens.shape[2]
    shard_rows = w_first.shape[0]
    row_ids = position * shard_rows + jnp.arange(shard_rows, dtype=jnp.int32)
    keep_first = expand_rows(mask_first, row_ids, extent)
    keep_second = expand_rows(mask_second, row_ids, extent)
    local_first = (w_first.astype(jnp.float32) * keep_first).astype(jnp.bfloat16)
    local_second = (w_second.astype(jnp.float32) * keep_second).astype(jnp.bfloat16)
    full = lax.all_gather(jnp.stack([local_first, local_second]), "seq", axis=1, tiled=True)
    full_first, full_second = full[0], full[1]
    shards = extent // shard_rows
    rows = tokens.shape[0]
    cols = cotangent.shape[1]
    flat_cot = lax.optimization_barrier(cotangent.reshape(extent, cols * channels))
    back_flat = lax.dot_general(
        full_second, flat_cot, (((0,), (0,)), ((), ())), preferred_element_type=jnp.float32
    ).astype(jnp.bfloat16)
    back_send = lax.optimization_barrier(back_flat.reshape(shards, rows, cols * channels))
    back_recv = lax.all_to_all(back_send, "seq", split_axis=0, concat_axis=0, tiled=True)
    tokens_late, back_send = lax.optimization_barrier((tokens, back_send))
    gate_full = gate_values.astype(jnp.float32)[:, :, None]
    gated = tokens_late.astype(jnp.float32) * gate_full
    hidden = jnp.einsum("ijc,kj->ikc", tokens_late, full_first, preferred_element_type=jnp.float32)
    mixed = (hidden * gated).astype(jnp.bfloat16)
    mixed_send = mixed.reshape(rows, shards, cols * channels).transpose(1, 0, 2)
    mixed_send, back_recv = lax.optimization_barrier((mixed_send, back_recv))
    flat_cols = lax.all_to_all(mixed_send, "seq", split_axis=0, concat_axis=0, tiled=True)
    back_rows = (
        back_recv.reshape(shards, rows, cols, channels).transpose(1, 0, 2, 3).reshape(tokens.shape)
    )
    back_float = back_rows.astype(jnp.float32)
    back_hidden = (back_float * gated).astype(jnp.bfloat16)
    direct = gate_full * back_float * hidden
    through = jnp.einsum("ikc,kj->ijc", back_hidden, full_first, preferred_element_type=jnp.float32)
    grad_tokens = (direct + through).astype(jnp.bfloat16)
    part_first = jnp.einsum(
        "ikc,ijc->kj", back_hidden, tokens_late, preferred_element_type=jnp.float32
    )
    summed_first = lax.psum_scatter(part_first, "seq", scatter_dimension=0, tiled=True)
    flat_cols, grad_tokens, part_first = lax.optimization_barrier(
        (flat_cols, grad_tokens, part_first)
    )
    part_second = lax.dot_general(
        flat_cot,
        flat_cols.reshape(extent, cols * channels),
        (((1,), (1,)), ((), ())),
        preferred_element_type=jnp.float32,
    )
    spread = lax.all_to_all(
        part_second.reshape(shards, shard_rows, extent), "seq", split_axis=0, concat_axis=0, tiled=True
    )
    summed_second = jnp.sum(spread, axis=0)
    factor = 1.0 / math.sqrt(extent * channels)
    grad_first = keep_first * summed_first * factor
    grad_second = keep_second * summed_second * factor
    return (grad_tokens, grad_first, grad_second)


def solution(mesh):
    in_specs = (
        P(("groups", "seq"), None, None),
        P("groups", "seq", None),
        P("seq", None),
        P("seq", None),
        P(),
        P(),
        P(("groups", "seq"), None),
    )
    out_specs = (
        P(("groups", "seq"), None, None),
        P(("groups", "seq"), None),
        P(("groups", "seq"), None),
    )
    return jax.shard_map(
        per_device, mesh=mesh, in_specs=in_specs, out_specs=out_specs, check_vma=False
    )
```

```python
import math

import jax
import jax.numpy as jnp
from jax import lax
from jax.sharding import PartitionSpec as P

BLK = 128


def expand_rows(mask, row_ids, extent):
    labels = jnp.arange(mask.shape[0], dtype=jnp.int32)
    row_pick = ((row_ids // BLK)[:, None] == labels[None, :]).astype(jnp.float32)
    col_pick = ((jnp.arange(extent, dtype=jnp.int32) // BLK)[:, None] == labels[None, :]).astype(
        jnp.float32
    )
    return jnp.dot(jnp.dot(row_pick, mask.astype(jnp.float32)), col_pick.T)


def per_device(tokens, cotangent, w_first, w_second, mask_first, mask_second, gate_values):
    position = lax.axis_index("seq")
    extent = tokens.shape[1]
    channels = tokens.shape[2]
    shard_rows = w_first.shape[0]
    row_ids = position * shard_rows + jnp.arange(shard_rows, dtype=jnp.int32)
    keep_first = expand_rows(mask_first, row_ids, extent)
    keep_second = expand_rows(mask_second, row_ids, extent)
    local_first = (w_first.astype(jnp.float32) * keep_first).astype(jnp.bfloat16)
    local_second = (w_second.astype(jnp.float32) * keep_second).astype(jnp.bfloat16)
    full = lax.all_gather(jnp.stack([local_first, local_second]), "seq", axis=1, tiled=True)
    full_first, full_second = full[0], full[1]
    shards = extent // shard_rows
    rows = tokens.shape[0]
    cols = cotangent.shape[1]
    flat_cot = lax.optimization_barrier(cotangent.reshape(extent, cols * channels))
    back_flat = lax.dot_general(
        full_second, flat_cot, (((0,), (0,)), ((), ())), preferred_element_type=jnp.float32
    ).astype(jnp.bfloat16)
    back_send = lax.optimization_barrier(back_flat.reshape(shards, rows, cols * channels))
    back_recv = lax.all_to_all(back_send, "seq", split_axis=0, concat_axis=0, tiled=True)
    tokens_late, back_send = lax.optimization_barrier((tokens, back_send))
    gate_full = gate_values.astype(jnp.float32)[:, :, None]
    gated = tokens_late.astype(jnp.float32) * gate_full
    hidden = jnp.einsum("ijc,kj->ikc", tokens_late, full_first, preferred_element_type=jnp.float32)
    mixed = (hidden * gated).astype(jnp.bfloat16)
    mixed_send = mixed.reshape(rows, shards, cols * channels).transpose(1, 0, 2)
    mixed_send, back_recv = lax.optimization_barrier((mixed_send, back_recv))
    flat_cols = lax.all_to_all(mixed_send, "seq", split_axis=0, concat_axis=0, tiled=True)
    back_rows = (
        back_recv.reshape(shards, rows, cols, channels).transpose(1, 0, 2, 3).reshape(tokens.shape)
    )
    back_float = back_rows.astype(jnp.float32)
    back_hidden = (back_float * gated).astype(jnp.bfloat16)
    direct = gate_full * back_float * hidden
    through = jnp.einsum("ikc,kj->ijc", back_hidden, full_first, preferred_element_type=jnp.float32)
    grad_tokens = (direct + through).astype(jnp.bfloat16)
    part_first = jnp.einsum(
        "ikc,ijc->kj", back_hidden, tokens_late, preferred_element_type=jnp.float32
    )
    summed_first = lax.psum_scatter(part_first, "seq", scatter_dimension=0, tiled=True)
    flat_cols, grad_tokens, summed_first = lax.optimization_barrier(
        (flat_cols, grad_tokens, summed_first)
    )
    part_second = lax.dot_general(
        flat_cot,
        flat_cols.reshape(extent, cols * channels),
        (((1,), (1,)), ((), ())),
        preferred_element_type=jnp.float32,
    )
    spread = lax.all_to_all(
        part_second.reshape(shards, shard_rows, extent), "seq", split_axis=0, concat_axis=0, tiled=True
    )
    summed_second = jnp.sum(spread, axis=0)
    factor = 1.0 / math.sqrt(extent * channels)
    grad_first = keep_first * summed_first * factor
    grad_second = keep_second * summed_second * factor
    return (grad_tokens, grad_first, grad_second)


def solution(mesh):
    in_specs = (
        P(("groups", "seq"), None, None),
        P("groups", "seq", None),
        P("seq", None),
        P("seq", None),
        P(),
        P(),
        P(("groups", "seq"), None),
    )
    out_specs = (
        P(("groups", "seq"), None, None),
        P(("groups", "seq"), None),
        P(("groups", "seq"), None),
    )
    return jax.shard_map(
        per_device, mesh=mesh, in_specs=in_specs, out_specs=out_specs, check_vma=False
    )
```
